256 devices in a mesh: phase: 4 (over x), ctx: 64 (over z, y, core).
Axes of the slice: x: 4, y: 4, z: 8, core: 2. Of those that a mesh axis runs over, the one named last changes fastest.
Arguments:
- hidden: bfloat16 [4, 8192, 4096], P('phase', 'ctx'), may hold values from -6 to 6
- queries: bfloat16 [4, 8192, 2048], P('phase', 'ctx'), may hold values from -400 to 400
- key_value_weight: bfloat16 [4, 4096, 1024], P('phase'), may hold values from -0.09375 to 0.09375
- doc_ids: int32 [4, 8192], P('phase'), may hold values from 0 to 7, never falling along the last dimension, each value on 1 to 6144 neighbouring positions
- scored: int32 [4, 8192], P('phase', 'ctx'), may hold values 0 or 1
Outputs:
- passed: bfloat16 [4, 8192, 2048], P('phase', 'ctx')
The draws below stay inside these ranges and needn't reach their ends.
Inputs may be any that keep to these rules, and one draw needn't show every extreme that they name: doc_ids never fall along a sequence; one document spans exactly 6144 tokens.
All inputs are finite; a program needn't handle non-finite values. No bound on the sum of `scored` on one device may be relied on, other than what follows from the above.
Results may differ from the reference program's by a relative error of at most 0.008.
The reference program's roundings to bfloat16 on the way count: a program that leaves them out, or rounds other values in their place, can miss the bound.
Values may be sent and summed in bfloat16 or wider, within the bound.
A program may use at most 128 MiB of HBM per device.

```python
import math
import jax
import jax.numpy as jnp
import numpy as np
from jax import lax

MODEL_WIDTH = 4096
QUERY_HEADS = 16
KEY_VALUE_HEADS = 4
HEAD_SIZE = 128
DOCS = 8
RELAY_SECTIONS = 4
SEQUENCE_TOKENS = 8192


def draw_queries(key, part):
    base = jnp.clip(jax.random.normal(key, (RELAY_SECTIONS, SEQUENCE_TOKENS, QUERY_HEADS * HEAD_SIZE), jnp.float32), -6.0, 6.0)
    return base.astype(jnp.bfloat16)


def plant(entries, own_key, low, largest):
    shape = entries.shape
    spot = [jax.random.randint(jax.random.fold_in(own_key, axis), (), 0, shape[axis]) for axis in range(len(shape))]
    entries = entries.at[tuple(spot)].set(low)
    longest = shape.index(max(shape))
    spot[longest] = (spot[longest] + 1) % shape[longest]
    return entries.at[tuple(spot)].set(largest)


def levels(rng, extent, pieces, low, high):
    def one(axis_at, parts):
        draws = jax.random.uniform(jax.random.fold_in(jax.random.fold_in(rng, 6), axis_at), (parts,), jnp.float32, low / len(pieces), high / len(pieces))
        return jnp.repeat(jnp.exp(draws), extent[axis_at] // parts).reshape((-1,) + (1,) * (len(extent) - axis_at - 1))

    level = one(*pieces[0])
    for cut in pieces[1:]:
        level = level * one(*cut)
    return level


def profile(count, total, limit, slope):
    portions = [(1 << 20) // math.isqrt(rank ** slope) + 1 for rank in range(2, count + 1)]
    spare, holding = total - limit - (count - 1), [1] * (count - 1)
    while spare > 0:
        free = [i for i in range(count - 1) if holding[i] < limit]
        mass, left = sum([portions[i] for i in free]), spare
        for i in free:
            extra = min(limit - holding[i], max(1, left * portions[i] // mass), spare)
            holding[i] = holding[i] + extra
            spare = spare - extra
    return np.array([limit] + holding)


def ragged(own_key, count, total, limit, slope):
    if count == 2:
        one = jax.random.randint(own_key, (), max(1, total - limit), min(limit, total - 1) + 1)
        return jnp.stack([one, total - one])
    tallies = jnp.asarray(profile(count, total, limit, slope), jnp.int32)
    pairs = (count - 1) // 2
    donor, taker = tallies[1:1 + 2 * pairs:2], tallies[2:2 + 2 * pairs:2]
    room = jnp.minimum(donor - 1, limit - taker)
    moved = jax.random.randint(jax.random.fold_in(own_key, 1), (pairs,), 0, 1 << 20) % (room + 1)
    tallies = tallies.at[1:1 + 2 * pairs:2].set(donor - moved).at[2:2 + 2 * pairs:2].set(taker + moved)
    return tallies[jax.random.permutation(jax.random.fold_in(own_key, 2), count)]


def normal_values(rng, dims, scale, reach, split=(), kind=jnp.bfloat16):
    array = jax.random.normal(rng, dims, jnp.float32) * scale
    if len(split) > 0:
        array = levels(rng, dims, split, -0.22, 0.18) * array
    return jnp.clip(array, min=-reach, max=reach).astype(kind)


def setup_inputs(seed: int = 0) -> dict:
    seeds = jax.random.split(jax.random.key(seed), 6)
    return {
        "hidden": normal_values(seeds[0], (RELAY_SECTIONS, SEQUENCE_TOKENS, MODEL_WIDTH), 1.0, 6.0, ((0, 4), (1, 64))),
        "queries": draw_queries(jax.random.fold_in(seeds[5], 71), 0),
        "key_value_weight": normal_values(seeds[2], (RELAY_SECTIONS, MODEL_WIDTH, 2 * KEY_VALUE_HEADS * HEAD_SIZE), MODEL_WIDTH ** -0.5, 0.09375, ((0, 4),)),
        "doc_ids": jax.vmap(lambda own: jnp.searchsorted(jnp.cumsum(ragged(own, DOCS, SEQUENCE_TOKENS, SEQUENCE_TOKENS * 3 // 4, 2)), jnp.arange(SEQUENCE_TOKENS), side="right"))(jax.random.split(seeds[3], RELAY_SECTIONS)).reshape((RELAY_SECTIONS, SEQUENCE_TOKENS)).astype(jnp.int32),
        "scored": plant((jax.random.randint(seeds[4], (RELAY_SECTIONS, SEQUENCE_TOKENS), 0, 4) < 3).astype(jnp.int32), jax.random.fold_in(seeds[4], 1), 0, 1),
    }


rope_base = 500000.0

def apply_rotary(key_heads, token_positions):
    half_dim = key_heads.shape[-1] // 2
    frequency = rope_base ** (-jnp.arange(half_dim, dtype=jnp.float32) * 2.0 / key_heads.shape[-1])
    angles = token_positions.astype(jnp.float32)[:, None] * frequency[None, :]
    cosine_part = jnp.cos(angles)[:, None, :]
    sine_part = jnp.sin(angles)[:, None, :]
    lower_half = key_heads[..., :half_dim]
    upper_half = key_heads[..., half_dim:]
    return jnp.concatenate([lower_half * cosine_part - upper_half * sine_part, upper_half * cosine_part + lower_half * sine_part], axis=-1)

def one_phase(hidden_rows, query_rows, weight_rows, doc_rows, mask_rows):
    wide = hidden_rows.astype(jnp.float32)
    normed = (wide * lax.rsqrt(lax.optimization_barrier(jnp.mean(wide * wide, axis=-1, keepdims=True)) + 1e-05)).astype(jnp.bfloat16)
    projected_rows = jnp.dot(normed, weight_rows, preferred_element_type=jnp.float32)
    key_value_width = KEY_VALUE_HEADS * HEAD_SIZE
    token_positions = jnp.arange(SEQUENCE_TOKENS, dtype=jnp.int32)
    key_matrix = apply_rotary(projected_rows[:, :key_value_width].reshape(SEQUENCE_TOKENS, KEY_VALUE_HEADS, HEAD_SIZE), token_positions).astype(jnp.bfloat16)
    value_matrix = projected_rows[:, key_value_width:].reshape(SEQUENCE_TOKENS, KEY_VALUE_HEADS, HEAD_SIZE).astype(jnp.bfloat16)
    query_group_width = QUERY_HEADS // KEY_VALUE_HEADS
    key_wide = jnp.repeat(key_matrix.astype(jnp.float32), query_group_width, axis=1)
    value_wide = jnp.repeat(value_matrix.astype(jnp.float32), query_group_width, axis=1)
    block_len = math.gcd(SEQUENCE_TOKENS, 256)
    score_scale = 1.0 / math.sqrt(HEAD_SIZE)

    def attend(offset):
        query_block = lax.dynamic_slice_in_dim(query_rows, offset, block_len, 0).astype(jnp.float32).reshape(block_len, QUERY_HEADS, HEAD_SIZE)
        scores = jnp.einsum('qhd,khd->hqk', query_block, key_wide) * score_scale
        query_pos = offset + jnp.arange(block_len, dtype=jnp.int32)
        query_doc = lax.dynamic_slice_in_dim(doc_rows, offset, block_len, 0)
        allowed = (token_positions[None, :] <= query_pos[:, None]) & (doc_rows[None, :] == query_doc[:, None])
        scores = jnp.where(allowed[None], scores, jnp.float32(-1e+30))
        row_max = lax.optimization_barrier(jnp.max(scores, axis=-1, keepdims=True))
        expo = jnp.exp(scores - row_max)
        total = lax.optimization_barrier(jnp.sum(expo, axis=-1))
        weights = expo.astype(jnp.bfloat16)
        result = jnp.einsum('hqk,khd->hqd', weights.astype(jnp.float32), value_wide) / total[..., None]
        return jnp.transpose(result, (1, 0, 2)).reshape(block_len, QUERY_HEADS * HEAD_SIZE)
    starts = jnp.arange(SEQUENCE_TOKENS // block_len, dtype=jnp.int32) * block_len
    attended = lax.map(attend, starts).reshape(SEQUENCE_TOKENS, QUERY_HEADS * HEAD_SIZE)
    return (attended * mask_rows.astype(jnp.float32)[:, None]).astype(jnp.bfloat16)

def reference(hidden, queries, key_value_weight, doc_ids, scored):
    outputs = [one_phase(hidden[phase_idx], queries[phase_idx], key_value_weight[phase_idx], doc_ids[phase_idx], scored[phase_idx]) for phase_idx in range(RELAY_SECTIONS)]
    return jnp.roll(jnp.stack(outputs, axis=0), 1, axis=0)
```

```python
import functools
import math

import jax
import jax.numpy as jnp
from jax import lax
from jax.experimental import pallas as pl
from jax.experimental.pallas import tpu as pltpu
from jax.sharding import PartitionSpec as P

KEY_VALUE_HEADS = 4
GROUP = 4
HEAD_SIZE = 128
ROPE_BASE = 500000.0
PHASES = 4
NZ, NY, NC = 8, 4, 2
ROWS = 128
MODEL_WIDTH = 4096
DEPTH_STEP = 1024
MESH = pl.DeviceIdType.MESH
FAR = -float(2.0**100)
SCALE = 1.0 / math.sqrt(HEAD_SIZE)
ANY = pl.BlockSpec(memory_space=pl.ANY)
VMEM = pl.BlockSpec(memory_space=pltpu.VMEM)


def project(hidden_ref, weight_ref, cos_ref, sin_ref, out_ref, normed, acc):
    step = pl.program_id(0)

    @pl.when(step == 0)
    def _():
        wide = hidden_ref[0].astype(jnp.float32)
        scale = lax.rsqrt(jnp.mean(wide * wide, axis=-1, keepdims=True) + 1e-05)
        rows = (wide * scale).astype(jnp.bfloat16)
        for i in range(MODEL_WIDTH // DEPTH_STEP):
            normed[i] = rows[:, i * DEPTH_STEP : (i + 1) * DEPTH_STEP]
        acc[...] = jnp.zeros_like(acc)

    acc[...] += jnp.dot(normed[step], weight_ref[0], preferred_element_type=jnp.float32)

    @pl.when(step == pl.num_programs(0) - 1)
    def _():
        cos, sin = cos_ref[...], sin_ref[...]
        half = HEAD_SIZE // 2
        for h in range(KEY_VALUE_HEADS):
            keys = acc[:, h * HEAD_SIZE : (h + 1) * HEAD_SIZE]
            low, high = keys[:, :half], keys[:, half:]
            turned = jnp.concatenate([low * cos - high * sin, high * cos + low * sin], axis=-1)
            out_ref[h, 0] = jnp.transpose(turned).astype(jnp.bfloat16)
            at = (KEY_VALUE_HEADS + h) * HEAD_SIZE
            out_ref[h, 1] = acc[:, at : at + HEAD_SIZE].astype(jnp.bfloat16)


def place():
    x = lax.axis_index("phase")
    at = lax.axis_index("ctx")
    z = at // (NY * NC)
    y = lax.rem(at // NC, NY)
    c = lax.rem(at, NC)
    return x, z, y, c


def device(x, z, y, c):
    return (x, (z * NY + y) * NC + c)


def gather(
    kvp, q, docs, scored, kv, q4, docs_out, scored_out,
    a_send, a_recv, q_send, q_recv, s_send, s_recv, up_send, up_recv, dn_send, dn_recv, p_send, p_recv,
):
    x, z, y, c = place()
    xn, xp = lax.rem(x + 1, PHASES), lax.rem(x + PHASES - 1, PHASES)
    zu, zd = lax.rem(z + 1, NZ), lax.rem(z + NZ - 1, NZ)
    barrier = pltpu.get_barrier_semaphore()
    for y2 in range(NY):
        pl.semaphore_signal(barrier, inc=1, device_id=device(xp, z, y2, c), device_id_type=MESH)
    for who in (device(x, zu, y, c), device(x, zd, y, c), device(x, z, y, 1 - c)):
        pl.semaphore_signal(barrier, inc=1, device_id=who, device_id_type=MESH)
    pl.semaphore_wait(barrier, NY + 3)

    def remote(src, dst, send, recv, who):
        return pltpu.make_async_remote_copy(
            src_ref=src, dst_ref=dst, send_sem=send, recv_sem=recv, device_id=who, device_id_type=MESH
        )

    started = []

    def go(copy):
        copy.start()
        started.append(copy)
        return copy

    first = [
        go(remote(kvp.at[h], kv.at[c, z, y], a_send.at[h], a_recv.at[y], device(xn, z, h, c)))
        for h in range(NY)
    ]
    small = [
        go(remote(docs, docs_out, s_send.at[0], s_recv.at[0], device(xn, z, y, c))),
        go(remote(scored, scored_out, s_send.at[1], s_recv.at[1], device(xn, z, y, c))),
    ]
    asked = [
        go(
            remote(
                q.at[0, :, pl.ds(h * GROUP * HEAD_SIZE, GROUP * HEAD_SIZE)],
                q4.at[y], q_send.at[h], q_recv.at[y], device(xn, z, h, c),
            )
        )
        for h in range(NY)
    ]

    def slot(r, p):
        return kv.at[c, lax.rem(z + r + NZ, NZ), p]

    def arrived(ref, sem):
        remote(ref, ref, sem, sem, device(x, z, y, 1 - c)).wait_recv()

    def partner(r, p):
        ref = slot(r, p)
        i = (r + NZ) % NZ
        go(remote(ref, ref, p_send.at[i, p], p_recv.at[i, p], device(x, z, y, 1 - c)))

    def up(k, p):
        ref = slot(-(k - 1), p)
        go(remote(ref, ref, up_send.at[k - 1, p], up_recv.at[k - 1, p], device(x, zu, y, c)))

    def down(k, p):
        ref = slot(k - 1, p)
        go(remote(ref, ref, dn_send.at[k - 1, p], dn_recv.at[k - 1, p], device(x, zd, y, c)))

    ups = {1: (0, 1, 2, 3), 2: (0, 1, 2, 3), 3: (0, 1, 2, 3), 4: (0, 1)}
    downs = {1: (0, 1, 2, 3), 2: (0, 1, 2, 3), 3: (0, 1, 2, 3), 4: (2, 3)}
    for p in range(NY):
        arrived(slot(0, p), a_recv.at[p])
        up(1, p)
        down(1, p)
        partner(0, p)
    for k in range(1, 5):
        for p in range(NY):
            if p in ups[k]:
                arrived(slot(-k, p), up_recv.at[k - 1, p])
                if k < 4 and p in ups[k + 1]:
                    up(k + 1, p)
                partner(-k, p)
            if p in downs[k]:
                arrived(slot(k, p), dn_recv.at[k - 1, p])
                if k < 4 and p in downs[k + 1]:
                    down(k + 1, p)
                partner(k, p)
    for r in range(NZ):
        for p in range(NY):
            arrived(kv.at[1 - c, lax.rem(z + r, NZ), p], p_recv.at[r, p])
    for p in range(NY):
        arrived(q4.at[p], q_recv.at[p])
    arrived(docs_out, s_recv.at[0])
    arrived(scored_out, s_recv.at[1])
    for copy in started:
        copy.wait_send()


CHUNK = NC * NY * ROWS


def attend(kv, q4, docs, out, qaug, kaug, vaug, acc, top):
    x, z, y, c = place()
    plane = NY * NC * ROWS
    lanes = lax.broadcasted_iota(jnp.int32, (ROWS, ROWS), 1)
    sublanes = lax.broadcasted_iota(jnp.int32, (ROWS, ROWS), 0)
    apart = jnp.where(lanes == sublanes, 0.0, FAR).astype(jnp.bfloat16)
    for j in range(NY):
        at = pl.multiple_of(z * plane + (j * NC + c) * ROWS, ROWS)
        mine = docs[:, pl.ds(at, ROWS)]
        hot = (sublanes == mine).astype(jnp.bfloat16)
        away = lax.dot_general(
            hot, apart, (((0,), (0,)), ((), ())), preferred_element_type=jnp.float32
        ).astype(jnp.bfloat16)
        for g in range(GROUP):
            r = (j * GROUP + g) * ROWS
            qaug[r : r + ROWS, :HEAD_SIZE] = q4[j, :, g * HEAD_SIZE : (g + 1) * HEAD_SIZE]
            qaug[r : r + ROWS, HEAD_SIZE:] = away
    vaug[:, HEAD_SIZE:] = jnp.ones((CHUNK, HEAD_SIZE), jnp.bfloat16)

    def load(zk):
        for c2 in range(NC):
            for p in range(NY):
                i = (c2 * NY + p) * ROWS
                kaug[:HEAD_SIZE, i : i + ROWS] = kv[c2, zk, p, 0]
                at = pl.multiple_of(zk * plane + (p * NC + c2) * ROWS, ROWS)
                kaug[HEAD_SIZE:, i : i + ROWS] = (sublanes == docs[:, pl.ds(at, ROWS)]).astype(jnp.bfloat16)
                vaug[i : i + ROWS, :HEAD_SIZE] = kv[c2, zk, p, 1]

    unit = 2 * ROWS

    def scores_of(rows):
        return jnp.dot(qaug[rows, :], kaug[...], preferred_element_type=jnp.float32)

    load(z)

    @pl.loop(0, NY * GROUP * ROWS // unit)
    def _(u):
        rows = pl.ds(pl.multiple_of(u * unit, unit), unit)
        s = scores_of(rows)
        key = lax.broadcasted_iota(jnp.int32, (1, CHUNK), 1)
        key = (lax.rem(key // ROWS, NY) * NC + key // (NY * ROWS)) * ROWS + lax.rem(key, ROWS)
        row = lax.broadcasted_iota(jnp.int32, (unit, 1), 0)
        own = (u // 2 * NC + c) * ROWS + lax.rem(row, ROWS)
        s = jnp.where(key <= own, s, -1e30)
        m = jnp.max(s, axis=-1, keepdims=True)
        w = jnp.exp((s - m) * SCALE).astype(jnp.bfloat16)
        acc[rows, :] = jnp.dot(w, vaug[...], preferred_element_type=jnp.float32)
        top[rows, :] = jnp.broadcast_to(m, (unit, HEAD_SIZE))

    at = pl.multiple_of(z * plane, ROWS)
    head_doc = docs[:, pl.ds(at, ROWS)][:, :1]
    start = jnp.sum((docs[...] < head_doc).astype(jnp.int32))

    @pl.loop(start // plane, z)
    def _(zk):
        load(zk)

        @pl.loop(0, NY * GROUP * ROWS // unit)
        def _(u):
            rows = pl.ds(pl.multiple_of(u * unit, unit), unit)
            s = scores_of(rows)
            before = top[rows, :1]
            m = jnp.maximum(before, jnp.max(s, axis=-1, keepdims=True))
            w = jnp.exp((s - m) * SCALE).astype(jnp.bfloat16)
            fade = jnp.exp((before - m) * SCALE)
            acc[rows, :] = acc[rows, :] * fade + jnp.dot(w, vaug[...], preferred_element_type=jnp.float32)
            top[rows, :] = jnp.broadcast_to(m, (unit, HEAD_SIZE))

    for j in range(NY):
        for g in range(GROUP):
            r = (j * GROUP + g) * ROWS
            out[j, :, g * HEAD_SIZE : (g + 1) * HEAD_SIZE] = (
                acc[r : r + ROWS, :HEAD_SIZE] / acc[r : r + ROWS, HEAD_SIZE:]
            ).astype(jnp.bfloat16)


def give_back(o, out, send, recv, local):
    x, z, y, c = place()
    barrier = pltpu.get_barrier_semaphore()
    for d in range(1, NY):
        pl.semaphore_signal(
            barrier, inc=1, device_id=device(x, z, lax.rem(y + d, NY), c), device_id_type=MESH
        )
    pl.semaphore_wait(barrier, NY - 1)
    keep = pltpu.make_async_copy(o.at[y], out.at[y], local)
    copies = []
    for d in (2, 1, 3):
        to = lax.rem(y + d, NY)
        copy = pltpu.make_async_remote_copy(
            src_ref=o.at[to], dst_ref=out.at[y], send_sem=send.at[d - 1], recv_sem=recv.at[d - 1],
            device_id=device(x, z, to, c), device_id_type=MESH,
        )
        copy.start()
        copies.append(copy)
    keep.start()
    keep.wait()
    for copy in copies:
        copy.wait()


def per_device(hidden, queries, key_value_weight, doc_ids, scored):
    first_row = lax.axis_index("ctx") * ROWS
    positions = first_row + jnp.arange(ROWS, dtype=jnp.int32)
    half = HEAD_SIZE // 2
    frequency = ROPE_BASE ** (-jnp.arange(half, dtype=jnp.float32) * 2.0 / HEAD_SIZE)
    angles = positions.astype(jnp.float32)[:, None] * frequency[None, :]
    kvp = pl.pallas_call(
        project,
        grid=(MODEL_WIDTH // DEPTH_STEP,),
        in_specs=[
            pl.BlockSpec((1, ROWS, MODEL_WIDTH), lambda i: (0, 0, 0)),
            pl.BlockSpec((1, DEPTH_STEP, 1024), lambda i: (0, i, 0)),
            pl.BlockSpec((ROWS, half), lambda i: (0, 0)),
            pl.BlockSpec((ROWS, half), lambda i: (0, 0)),
        ],
        out_specs=pl.BlockSpec((NY, 2, ROWS, HEAD_SIZE), lambda i: (0, 0, 0, 0)),
        out_shape=jax.ShapeDtypeStruct((NY, 2, ROWS, HEAD_SIZE), jnp.bfloat16),
        scratch_shapes=[
            pltpu.VMEM((MODEL_WIDTH // DEPTH_STEP, ROWS, DEPTH_STEP), jnp.bfloat16),
            pltpu.VMEM((ROWS, 1024), jnp.float32),
        ],
        name="project",
    )(hidden, key_value_weight, jnp.cos(angles), jnp.sin(angles))

    dma = pltpu.SemaphoreType.DMA
    kv, q4, docs, marks = pl.pallas_call(
        gather,
        in_specs=[ANY] * 4,
        out_specs=[ANY] * 4,
        out_shape=[
            jax.ShapeDtypeStruct((NC, NZ, NY, 2, ROWS, HEAD_SIZE), jnp.bfloat16),
            jax.ShapeDtypeStruct((NY, ROWS, GROUP * HEAD_SIZE), jnp.bfloat16),
            jax.ShapeDtypeStruct(doc_ids.shape, jnp.int32),
            jax.ShapeDtypeStruct(scored.shape, jnp.int32),
        ],
        scratch_shapes=[
            dma((NY,)), dma((NY,)), dma((NY,)), dma((NY,)), dma((2,)), dma((2,)),
            dma((4, NY)), dma((4, NY)), dma((4, NY)), dma((4, NY)), dma((NZ, NY)), dma((NZ, NY)),
        ],
        compiler_params=pltpu.CompilerParams(collective_id=0, has_side_effects=True),
        name="gather",
    )(kvp, queries, doc_ids, scored)

    o = pl.pallas_call(
        attend,
        in_specs=[VMEM] * 3,
        out_specs=VMEM,
        out_shape=jax.ShapeDtypeStruct((NY, ROWS, GROUP * HEAD_SIZE), jnp.bfloat16),
        scratch_shapes=[
            pltpu.VMEM((NY * GROUP * ROWS, 2 * HEAD_SIZE), jnp.bfloat16),
            pltpu.VMEM((2 * HEAD_SIZE, CHUNK), jnp.bfloat16),
            pltpu.VMEM((CHUNK, 2 * HEAD_SIZE), jnp.bfloat16),
            pltpu.VMEM((NY * GROUP * ROWS, 2 * HEAD_SIZE), jnp.float32),
            pltpu.VMEM((NY * GROUP * ROWS, HEAD_SIZE), jnp.float32),
        ],
        name="attend",
    )(kv, q4, docs)

    back = pl.pallas_call(
        give_back,
        in_specs=[ANY],
        out_specs=ANY,
        out_shape=jax.ShapeDtypeStruct((NY, ROWS, GROUP * HEAD_SIZE), jnp.bfloat16),
        scratch_shapes=[dma((NY - 1,)), dma((NY - 1,)), dma],
        compiler_params=pltpu.CompilerParams(collective_id=1, has_side_effects=True),
        name="give_back",
    )(o)
    flat = jnp.transpose(back, (1, 0, 2)).reshape(ROWS, NY * GROUP * HEAD_SIZE)
    return (flat * marks[0].astype(jnp.bfloat16)[:, None])[None]


def solution(mesh):
    placed = (
        P("phase", "ctx", None),
        P("phase", "ctx", None),
        P("phase", None, None),
        P("phase", None),
        P("phase", "ctx"),
    )
    return jax.shard_map(
        per_device, mesh=mesh, in_specs=placed, out_specs=P("phase", "ctx", None), check_vma=False
    )
```

```python
import math

import jax
import jax.numpy as jnp
from jax import lax
from jax.experimental import pallas as pl
from jax.experimental.pallas import tpu as pltpu
from jax.sharding import PartitionSpec as P

KEY_VALUE_HEADS = 4
HEAD_SIZE = 128
ROPE_BASE = 500000.0
PHASES = 4
NZ, NY, NC = 8, 4, 2
ROWS = 128
MODEL_WIDTH = 4096
DEPTH_STEP = 512
MESH = pl.DeviceIdType.MESH
FAR = -float(2.0**100)
SCALE = math.log2(math.e) / math.sqrt(HEAD_SIZE)
ORDER = (0, 1, 7, 2, 6, 3, 5, 4)
WIDTH = 2 * HEAD_SIZE
CHUNK = NC * NY * ROWS
ANY = pl.BlockSpec(memory_space=pl.ANY)
VMEM = pl.BlockSpec(memory_space=pltpu.VMEM)


def place():
    x = lax.axis_index("phase")
    at = lax.axis_index("ctx")
    z = at // (NY * NC)
    y = lax.rem(at // NC, NY)
    c = lax.rem(at, NC)
    return x, z, y, c


def device(x, z, y, c):
    return (x, (z * NY + y) * NC + c)


def remote(src, dst, send, recv, who):
    return pltpu.make_async_remote_copy(
        src_ref=src, dst_ref=dst, send_sem=send, recv_sem=recv, device_id=who, device_id_type=MESH
    )


def gather(
    hidden, weight, q, cos_ref, sin_ref, kv, q8,
    wbuf, kvp, acc, own, w_sem, l_sem,
    a_send, a_recv, q_send, q_recv, up_send, up_recv, dn_send, dn_recv, p_send, p_recv,
):
    x, z, y, c = place()
    yu, yd = lax.rem(y + 1, NY), lax.rem(y + NY - 1, NY)
    loads = []
    for i in range(MODEL_WIDTH // DEPTH_STEP):
        part = pl.ds(i * DEPTH_STEP, DEPTH_STEP)
        load = pltpu.make_async_copy(weight.at[0, part], wbuf.at[part], w_sem.at[i])
        load.start()
        loads.append(load)
    barrier = pltpu.get_barrier_semaphore()
    for d in range(1, NZ):
        pl.semaphore_signal(
            barrier, inc=1, device_id=device(x, lax.rem(z + d, NZ), y, c), device_id_type=MESH
        )
    for who in (device(x, z, yu, c), device(x, z, yd, c), device(x, z, y, 1 - c)):
        pl.semaphore_signal(barrier, inc=1, device_id=who, device_id_type=MESH)
    pl.semaphore_wait(barrier, NZ - 1 + 3)

    started = []

    def go(copy):
        copy.start()
        started.append(copy)

    def columns(at):
        return q.at[0, :, pl.ds(pl.multiple_of(at * WIDTH, WIDTH), WIDTH)]

    for d in ORDER[1:]:
        to = lax.rem(z + d, NZ)
        go(remote(columns(to), q8.at[z], q_send.at[d], q_recv.at[z], device(x, to, y, c)))
    keep = pltpu.make_async_copy(columns(z), own, l_sem.at[0])
    keep.start()

    wide = hidden[0].astype(jnp.float32)
    scale = lax.rsqrt(jnp.mean(wide * wide, axis=-1, keepdims=True) + 1e-05)
    rows = (wide * scale).astype(jnp.bfloat16)
    for i, load in enumerate(loads):
        load.wait()
        term = jnp.dot(
            rows[:, i * DEPTH_STEP : (i + 1) * DEPTH_STEP],
            wbuf[i * DEPTH_STEP : (i + 1) * DEPTH_STEP, :],
            preferred_element_type=jnp.float32,
        )
        if i == 0:
            acc[...] = term
        else:
            acc[...] += term
    cos, sin = cos_ref[...], sin_ref[...]
    half = HEAD_SIZE // 2
    for h in range(KEY_VALUE_HEADS):
        keys = acc[:, h * HEAD_SIZE : (h + 1) * HEAD_SIZE]
        low, high = keys[:, :half], keys[:, half:]
        turned = jnp.concatenate([low * cos - high * sin, high * cos + low * sin], axis=-1)
        kvp[h, 0] = jnp.transpose(turned).astype(jnp.bfloat16)
        at = (KEY_VALUE_HEADS + h) * HEAD_SIZE
        kvp[h, 1] = acc[:, at : at + HEAD_SIZE].astype(jnp.bfloat16)

    keep.wait()
    put = pltpu.make_async_copy(own, q8.at[z], l_sem.at[1])
    put.start()

    for d in ORDER[1:]:
        to = lax.rem(z + d, NZ)
        go(remote(kvp.at[to // 2], kv.at[c, y, z], a_send.at[d], a_recv.at[z], device(x, to, y, c)))
    mine = kvp.at[z // 2]
    home = pltpu.make_async_copy(mine, kv.at[c, y, z], l_sem.at[2])
    home.start()

    def slot(r, d):
        return kv.at[c, lax.rem(y + r + NY, NY), lax.rem(z + d, NZ)]

    def arrived(ref, sem):
        remote(ref, ref, sem, sem, device(x, z, y, 1 - c)).wait_recv()

    def partner(r, d, ref=None):
        i = (r + NY) % NY
        src = slot(r, d) if ref is None else ref
        go(remote(src, slot(r, d), p_send.at[i, d], p_recv.at[i, d], device(x, z, y, 1 - c)))

    def up(k, d, ref=None):
        dst = slot(1 - k, d)
        src = dst if ref is None else ref
        go(remote(src, dst, up_send.at[k - 1, d], up_recv.at[k - 1, d], device(x, z, yu, c)))

    def down(k, d, ref=None):
        dst = slot(k - 1, d)
        src = dst if ref is None else ref
        go(remote(src, dst, dn_send.at[k - 1, d], dn_recv.at[k - 1, d], device(x, z, yd, c)))

    far_up, far_down = ORDER[0::2], ORDER[1::2]
    for d in ORDER:
        if d == 0:
            up(1, d, mine)
            down(1, d, mine)
            partner(0, d, mine)
        else:
            arrived(slot(0, d), a_recv.at[lax.rem(z + d, NZ)])
            up(1, d)
            down(1, d)
            partner(0, d)
    for d in ORDER:
        arrived(slot(-1, d), up_recv.at[0, d])
        if d in far_up:
            up(2, d)
        partner(-1, d)
        arrived(slot(1, d), dn_recv.at[0, d])
        if d in far_down:
            down(2, d)
        partner(1, d)
    for d in ORDER:
        if d in far_up:
            arrived(slot(2, d), up_recv.at[1, d])
        else:
            arrived(slot(2, d), dn_recv.at[1, d])
        partner(2, d)
    for r in range(NY):
        for d in ORDER:
            arrived(kv.at[1 - c, lax.rem(y + r, NY), lax.rem(z + d, NZ)], p_recv.at[r, d])
    for d in ORDER[1:]:
        at = lax.rem(z + d, NZ)
        arrived(q8.at[at], q_recv.at[at])
    put.wait()
    home.wait()
    for copy in started:
        copy.wait_send()


UNIT = 2 * ROWS


def attend(kv, q8, docs, out, qaug, kaug, vaug, acc, top):
    x, z, y, c = place()
    lanes = lax.broadcasted_iota(jnp.int32, (ROWS, ROWS), 1)
    sublanes = lax.broadcasted_iota(jnp.int32, (ROWS, ROWS), 0)
    apart = jnp.where(lanes == sublanes, 0.0, FAR).astype(jnp.bfloat16)
    block = y * NC + c

    @pl.loop(0, NZ)
    def _(i):
        at = pl.multiple_of(i * CHUNK + block * ROWS, ROWS)
        hot = (sublanes == docs[:, pl.ds(at, ROWS)]).astype(jnp.bfloat16)
        away = lax.dot_general(
            hot, apart, (((0,), (0,)), ((), ())), preferred_element_type=jnp.float32
        ).astype(jnp.bfloat16)
        for g in range(2):
            qaug[i, g * ROWS : (g + 1) * ROWS, :HEAD_SIZE] = q8[i, :, g * HEAD_SIZE : (g + 1) * HEAD_SIZE]
            qaug[i, g * ROWS : (g + 1) * ROWS, HEAD_SIZE:] = away
        vaug[i, :, HEAD_SIZE:] = jnp.ones((CHUNK, HEAD_SIZE), jnp.bfloat16)
        for p in range(NY):
            for c2 in range(NC):
                b = (p * NC + c2) * ROWS
                at = pl.multiple_of(i * CHUNK + b, ROWS)
                kaug[i, :HEAD_SIZE, b : b + ROWS] = kv[c2, p, i, 0]
                kaug[i, HEAD_SIZE:, b : b + ROWS] = (sublanes == docs[:, pl.ds(at, ROWS)]).astype(jnp.bfloat16)
                vaug[i, b : b + ROWS, :HEAD_SIZE] = kv[c2, p, i, 1]

    def scores(i, k):
        return jnp.dot(qaug[i], kaug[k], preferred_element_type=jnp.float32)

    def first(i):
        s = scores(i, i)
        key = lax.broadcasted_iota(jnp.int32, (1, CHUNK), 1)
        row = lax.broadcasted_iota(jnp.int32, (UNIT, 1), 0)
        s = jnp.where(key <= block * ROWS + lax.rem(row, ROWS), s, -1e30)
        m = jnp.max(s, axis=-1, keepdims=True)
        w = jnp.exp2((s - m) * SCALE).astype(jnp.bfloat16)
        return m, jnp.dot(w, vaug[i], preferred_element_type=jnp.float32)

    def later(i, k, before):
        s = scores(i, k)
        m = jnp.maximum(before, jnp.max(s, axis=-1, keepdims=True))
        w = jnp.exp2((s - m) * SCALE).astype(jnp.bfloat16)
        return m, jnp.exp2((before - m) * SCALE), jnp.dot(w, vaug[k], preferred_element_type=jnp.float32)

    def keep(j, m, total):
        acc[j] = total
        top[j] = jnp.broadcast_to(m, (UNIT, HEAD_SIZE))

    @pl.loop(0, NZ // 2)
    def _(u):
        even, odd = 2 * u, 2 * u + 1
        m0, t0 = first(even)
        m1, t1 = first(odd)
        m1, fade, more = later(odd, even, m1)
        keep(0, m0, t0)
        keep(1, m1, t1 * fade + more)
        at = pl.multiple_of(even * CHUNK + block * ROWS, ROWS)
        head_doc = docs[:, pl.ds(at, ROWS)][:, :1]
        start = jnp.sum((docs[...] < head_doc).astype(jnp.int32))

        @pl.loop(start // CHUNK, even)
        def _(k):
            m0, f0, t0 = later(even, k, top[0][:, :1])
            m1, f1, t1 = later(odd, k, top[1][:, :1])
            keep(0, m0, acc[0] * f0 + t0)
            keep(1, m1, acc[1] * f1 + t1)

        for j in range(2):
            done = (acc[j][:, :HEAD_SIZE] / acc[j][:, HEAD_SIZE:]).astype(jnp.bfloat16)
            for g in range(2):
                out[2 * u + j, :, g * HEAD_SIZE : (g + 1) * HEAD_SIZE] = done[g * ROWS : (g + 1) * ROWS]


def give_back(o, scored, out, marks, send, recv, s_send, s_recv):
    x, z, y, c = place()
    xn, xp = lax.rem(x + 1, PHASES), lax.rem(x + PHASES - 1, PHASES)
    barrier = pltpu.get_barrier_semaphore()
    for d in range(NZ):
        pl.semaphore_signal(
            barrier, inc=1, device_id=device(xp, lax.rem(z + d, NZ), y, c), device_id_type=MESH
        )
    pl.semaphore_wait(barrier, NZ)
    started = []
    for d in reversed(ORDER):
        to = lax.rem(z + d, NZ)
        copy = remote(
            o.at[to], out.at[:, pl.ds(pl.multiple_of(z * WIDTH, WIDTH), WIDTH)],
            send.at[d], recv.at[z], device(xn, to, y, c),
        )
        copy.start()
        started.append(copy)
    copy = remote(scored, marks, s_send, s_recv, device(xn, z, y, c))
    copy.start()
    copy.wait()
    for d in range(NZ):
        at = lax.rem(z + d, NZ)
        ref = out.at[:, pl.ds(pl.multiple_of(at * WIDTH, WIDTH), WIDTH)]
        remote(ref, ref, send.at[d], recv.at[at], device(xn, z, y, c)).wait_recv()
    for copy in started:
        copy.wait_send()


def per_device(hidden, queries, key_value_weight, doc_ids, scored):
    first_row = lax.axis_index("ctx") * ROWS
    positions = first_row + jnp.arange(ROWS, dtype=jnp.int32)
    half = HEAD_SIZE // 2
    frequency = ROPE_BASE ** (-jnp.arange(half, dtype=jnp.float32) * 2.0 / HEAD_SIZE)
    angles = positions.astype(jnp.float32)[:, None] * frequency[None, :]
    dma = pltpu.SemaphoreType.DMA
    steps = MODEL_WIDTH // DEPTH_STEP
    kv, q8 = pl.pallas_call(
        gather,
        in_specs=[VMEM, ANY, ANY, VMEM, VMEM],
        out_specs=[ANY] * 2,
        out_shape=[
            jax.ShapeDtypeStruct((NC, NY, NZ, 2, ROWS, HEAD_SIZE), jnp.bfloat16),
            jax.ShapeDtypeStruct((NZ, ROWS, WIDTH), jnp.bfloat16),
        ],
        scratch_shapes=[
            pltpu.VMEM((MODEL_WIDTH, 1024), jnp.bfloat16),
            pltpu.VMEM((KEY_VALUE_HEADS, 2, ROWS, HEAD_SIZE), jnp.bfloat16),
            pltpu.VMEM((ROWS, 1024), jnp.float32),
            pltpu.VMEM((ROWS, WIDTH), jnp.bfloat16),
            dma((steps,)), dma((3,)),
            dma((NZ,)), dma((NZ,)), dma((NZ,)), dma((NZ,)),
            dma((2, NZ)), dma((2, NZ)), dma((2, NZ)), dma((2, NZ)), dma((NY, NZ)), dma((NY, NZ)),
        ],
        compiler_params=pltpu.CompilerParams(
            collective_id=0, has_side_effects=True, vmem_limit_bytes=40 << 20
        ),
        name="gather",
    )(hidden, key_value_weight, queries, jnp.cos(angles), jnp.sin(angles))

    o = pl.pallas_call(
        attend,
        in_specs=[VMEM] * 3,
        out_specs=VMEM,
        out_shape=jax.ShapeDtypeStruct((NZ, ROWS, WIDTH), jnp.bfloat16),
        scratch_shapes=[
            pltpu.VMEM((NZ, UNIT, 2 * HEAD_SIZE), jnp.bfloat16),
            pltpu.VMEM((NZ, 2 * HEAD_SIZE, CHUNK), jnp.bfloat16),
            pltpu.VMEM((NZ, CHUNK, 2 * HEAD_SIZE), jnp.bfloat16),
            pltpu.VMEM((2, UNIT, 2 * HEAD_SIZE), jnp.float32),
            pltpu.VMEM((2, UNIT, HEAD_SIZE), jnp.float32),
        ],
        compiler_params=pltpu.CompilerParams(vmem_limit_bytes=50 << 20),
        name="attend",
    )(kv, q8, doc_ids)

    back, marks = pl.pallas_call(
        give_back,
        in_specs=[ANY] * 2,
        out_specs=[ANY] * 2,
        out_shape=[
            jax.ShapeDtypeStruct((ROWS, NZ * WIDTH), jnp.bfloat16),
            jax.ShapeDtypeStruct(scored.shape, jnp.int32),
        ],
        scratch_shapes=[dma((NZ,)), dma((NZ,)), dma, dma],
        compiler_params=pltpu.CompilerParams(collective_id=1, has_side_effects=True),
        name="give_back",
    )(o, scored)
    return (back * marks[0].astype(jnp.bfloat16)[:, None])[None]


def solution(mesh):
    placed = (
        P("phase", "ctx", None),
        P("phase", "ctx", None),
        P("phase", None, None),
        P("phase", None),
        P("phase", "ctx"),
    )
    return jax.shard_map(
        per_device, mesh=mesh, in_specs=placed, out_specs=P("phase", "ctx", None), check_vma=False
    )
```

```python
import math

import jax
import jax.numpy as jnp
from jax import lax
from jax.experimental import pallas as pl
from jax.experimental.pallas import tpu as pltpu
from jax.sharding import PartitionSpec as P

KEY_VALUE_HEADS = 4
HEAD_SIZE = 128
ROPE_BASE = 500000.0
PHASES = 4
NZ, NY, NC = 8, 4, 2
ROWS = 128
MODEL_WIDTH = 4096
DEPTH_STEP = 512
MESH = pl.DeviceIdType.MESH
FAR = -float(2.0**100)
SCALE = math.log2(math.e) / math.sqrt(HEAD_SIZE)
ORDER = (0, 1, 7, 2, 6, 3, 5, 4)
WIDTH = 2 * HEAD_SIZE
CHUNK = NC * NY * ROWS
ANY = pl.BlockSpec(memory_space=pl.ANY)
VMEM = pl.BlockSpec(memory_space=pltpu.VMEM)


def place():
    x = lax.axis_index("phase")
    at = lax.axis_index("ctx")
    z = at // (NY * NC)
    y = lax.rem(at // NC, NY)
    c = lax.rem(at, NC)
    return x, z, y, c


def device(x, z, y, c):
    return (x, (z * NY + y) * NC + c)


def remote(src, dst, send, recv, who):
    return pltpu.make_async_remote_copy(
        src_ref=src, dst_ref=dst, send_sem=send, recv_sem=recv, device_id=who, device_id_type=MESH
    )


def gather(
    hidden, weight, q, cos_ref, sin_ref, kv, q8,
    wbuf, hbuf, kvp, acc, own, w_sem, l_sem,
    a_send, a_recv, q_send, q_recv, up_send, up_recv, dn_send, dn_recv, p_send, p_recv,
):
    x, z, y, c = place()
    yu, yd = lax.rem(y + 1, NY), lax.rem(y + NY - 1, NY)
    fetch = pltpu.make_async_copy(hidden.at[0], hbuf, l_sem.at[3])
    fetch.start()
    loads = []
    for i in range(MODEL_WIDTH // DEPTH_STEP):
        part = pl.ds(i * DEPTH_STEP, DEPTH_STEP)
        load = pltpu.make_async_copy(weight.at[0, part], wbuf.at[part], w_sem.at[i])
        load.start()
        loads.append(load)
    barrier = pltpu.get_barrier_semaphore()
    for d in range(1, NZ):
        pl.semaphore_signal(
            barrier, inc=1, device_id=device(x, lax.rem(z + d, NZ), y, c), device_id_type=MESH
        )
    for who in (device(x, z, yu, c), device(x, z, yd, c), device(x, z, y, 1 - c)):
        pl.semaphore_signal(barrier, inc=1, device_id=who, device_id_type=MESH)
    pl.semaphore_wait(barrier, NZ - 1 + 3)

    started = []

    def go(copy):
        copy.start()
        started.append(copy)

    def columns(at):
        return q.at[0, :, pl.ds(pl.multiple_of(at * WIDTH, WIDTH), WIDTH)]

    def ask(d):
        to = lax.rem(z + d, NZ)
        go(remote(columns(to), q8.at[z], q_send.at[d], q_recv.at[z], device(x, to, y, c)))

    for d in (4, 3, 5):
        ask(d)
    keep = pltpu.make_async_copy(columns(z), own, l_sem.at[0])
    keep.start()

    fetch.wait()
    wide = hbuf[...].astype(jnp.float32)
    scale = lax.rsqrt(jnp.mean(wide * wide, axis=-1, keepdims=True) + 1e-05)
    rows = (wide * scale).astype(jnp.bfloat16)
    for i, load in enumerate(loads):
        load.wait()
        term = jnp.dot(
            rows[:, i * DEPTH_STEP : (i + 1) * DEPTH_STEP],
            wbuf[i * DEPTH_STEP : (i + 1) * DEPTH_STEP, :],
            preferred_element_type=jnp.float32,
        )
        if i == 0:
            acc[...] = term
        else:
            acc[...] += term
    cos, sin = cos_ref[...], sin_ref[...]
    half = HEAD_SIZE // 2
    for h in range(KEY_VALUE_HEADS):
        keys = acc[:, h * HEAD_SIZE : (h + 1) * HEAD_SIZE]
        low, high = keys[:, :half], keys[:, half:]
        turned = jnp.concatenate([low * cos - high * sin, high * cos + low * sin], axis=-1)
        kvp[h, 0] = jnp.transpose(turned).astype(jnp.bfloat16)
        at = (KEY_VALUE_HEADS + h) * HEAD_SIZE
        kvp[h, 1] = acc[:, at : at + HEAD_SIZE].astype(jnp.bfloat16)

    keep.wait()
    put = pltpu.make_async_copy(own, q8.at[z], l_sem.at[1])
    put.start()

    for d in ORDER[1:]:
        to = lax.rem(z + d, NZ)
        go(remote(kvp.at[to // 2], kv.at[c, y, z], a_send.at[d], a_recv.at[z], device(x, to, y, c)))
    for d in (2, 6, 1, 7):
        ask(d)
    mine = kvp.at[z // 2]
    home = pltpu.make_async_copy(mine, kv.at[c, y, z], l_sem.at[2])
    home.start()

    def slot(r, d):
        return kv.at[c, lax.rem(y + r + NY, NY), lax.rem(z + d, NZ)]

    def arrived(ref, sem):
        remote(ref, ref, sem, sem, device(x, z, y, 1 - c)).wait_recv()

    def partner(r, d, ref=None):
        i = (r + NY) % NY
        src = slot(r, d) if ref is None else ref
        go(remote(src, slot(r, d), p_send.at[i, d], p_recv.at[i, d], device(x, z, y, 1 - c)))

    def up(k, d, ref=None):
        dst = slot(1 - k, d)
        src = dst if ref is None else ref
        go(remote(src, dst, up_send.at[k - 1, d], up_recv.at[k - 1, d], device(x, z, yu, c)))

    def down(k, d, ref=None):
        dst = slot(k - 1, d)
        src = dst if ref is None else ref
        go(remote(src, dst, dn_send.at[k - 1, d], dn_recv.at[k - 1, d], device(x, z, yd, c)))

    far_up, far_down = ORDER[0::2], ORDER[1::2]
    for d in ORDER:
        if d == 0:
            up(1, d, mine)
            down(1, d, mine)
            partner(0, d, mine)
        else:
            arrived(slot(0, d), a_recv.at[lax.rem(z + d, NZ)])
            up(1, d)
            down(1, d)
            partner(0, d)
    for d in ORDER:
        arrived(slot(-1, d), up_recv.at[0, d])
        if d in far_up:
            up(2, d)
        partner(-1, d)
        arrived(slot(1, d), dn_recv.at[0, d])
        if d in far_down:
            down(2, d)
        partner(1, d)
    for d in ORDER:
        if d in far_up:
            arrived(slot(2, d), up_recv.at[1, d])
        else:
            arrived(slot(2, d), dn_recv.at[1, d])
        partner(2, d)
    for r in range(NY):
        for d in ORDER:
            arrived(kv.at[1 - c, lax.rem(y + r, NY), lax.rem(z + d, NZ)], p_recv.at[r, d])
    for d in ORDER[1:]:
        at = lax.rem(z + d, NZ)
        arrived(q8.at[at], q_recv.at[at])
    put.wait()
    home.wait()
    for copy in started:
        copy.wait_send()


UNIT = 2 * ROWS


def attend(
    kv, q8, docs, scored, out, marks,
    qaug, kaug, vaug, acc, top, o, l_sem, send, recv, s_send, s_recv,
):
    x, z, y, c = place()
    xn, xp = lax.rem(x + 1, PHASES), lax.rem(x + PHASES - 1, PHASES)
    loads = []
    for p in range(NY):
        for c2 in range(NC):
            b = p * NC + c2
            keys = pl.ds(b * ROWS, ROWS)
            for part, dst in ((0, kaug.at[:, :HEAD_SIZE, keys]), (1, vaug.at[:, keys, :HEAD_SIZE])):
                load = pltpu.make_async_copy(kv.at[c2, p, :, part], dst, l_sem.at[2 * b + part])
                load.start()
                loads.append(load)
    barrier = pltpu.get_barrier_semaphore()
    for d in range(NZ):
        pl.semaphore_signal(
            barrier, inc=1, device_id=device(xp, lax.rem(z + d, NZ), y, c), device_id_type=MESH
        )
    lanes = lax.broadcasted_iota(jnp.int32, (ROWS, ROWS), 1)
    sublanes = lax.broadcasted_iota(jnp.int32, (ROWS, ROWS), 0)
    apart = jnp.where(lanes == sublanes, 0.0, FAR).astype(jnp.bfloat16)
    block = y * NC + c

    @pl.loop(0, NZ)
    def _(i):
        at = pl.multiple_of(i * CHUNK + block * ROWS, ROWS)
        hot = (sublanes == docs[:, pl.ds(at, ROWS)]).astype(jnp.bfloat16)
        away = lax.dot_general(
            hot, apart, (((0,), (0,)), ((), ())), preferred_element_type=jnp.float32
        ).astype(jnp.bfloat16)
        for g in range(2):
            qaug[i, g * ROWS : (g + 1) * ROWS, :HEAD_SIZE] = q8[i, :, g * HEAD_SIZE : (g + 1) * HEAD_SIZE]
            qaug[i, g * ROWS : (g + 1) * ROWS, HEAD_SIZE:] = away
        vaug[i, :, HEAD_SIZE:] = jnp.ones((CHUNK, HEAD_SIZE), jnp.bfloat16)
        for b in range(NY * NC):
            at = pl.multiple_of(i * CHUNK + b * ROWS, ROWS)
            kaug[i, HEAD_SIZE:, b * ROWS : (b + 1) * ROWS] = (
                sublanes == docs[:, pl.ds(at, ROWS)]
            ).astype(jnp.bfloat16)

    for load in loads:
        load.wait()
    pl.semaphore_wait(barrier, NZ)
    mark = remote(scored, marks, s_send, s_recv, device(xn, z, y, c))
    mark.start()

    def scores(i, k):
        return jnp.dot(qaug[i], kaug[k], preferred_element_type=jnp.float32)

    def first(i):
        s = scores(i, i)
        key = lax.broadcasted_iota(jnp.int32, (1, CHUNK), 1)
        row = lax.broadcasted_iota(jnp.int32, (UNIT, 1), 0)
        s = jnp.where(key <= block * ROWS + lax.rem(row, ROWS), s, -1e30)
        m = jnp.max(s, axis=-1, keepdims=True)
        w = jnp.exp2((s - m) * SCALE).astype(jnp.bfloat16)
        return m, jnp.dot(w, vaug[i], preferred_element_type=jnp.float32)

    def later(i, k, before):
        s = scores(i, k)
        m = jnp.maximum(before, jnp.max(s, axis=-1, keepdims=True))
        w = jnp.exp2((s - m) * SCALE).astype(jnp.bfloat16)
        return m, jnp.exp2((before - m) * SCALE), jnp.dot(w, vaug[k], preferred_element_type=jnp.float32)

    def keep(j, m, total):
        acc[j] = total
        top[j] = jnp.broadcast_to(m, (UNIT, HEAD_SIZE))

    mine = out.at[:, pl.ds(pl.multiple_of(z * WIDTH, WIDTH), WIDTH)]

    @pl.loop(0, NZ // 2)
    def _(n):
        u = lax.rem(z // 2 + n, NZ // 2)
        even, odd = 2 * u, 2 * u + 1
        m0, t0 = first(even)
        m1, t1 = first(odd)
        m1, fade, more = later(odd, even, m1)
        keep(0, m0, t0)
        keep(1, m1, t1 * fade + more)

        @pl.loop(0, even)
        def _(k):
            m0, f0, t0 = later(even, k, top[0][:, :1])
            m1, f1, t1 = later(odd, k, top[1][:, :1])
            keep(0, m0, acc[0] * f0 + t0)
            keep(1, m1, acc[1] * f1 + t1)

        for j in range(2):
            done = (acc[j][:, :HEAD_SIZE] / acc[j][:, HEAD_SIZE:]).astype(jnp.bfloat16)
            for g in range(2):
                o[2 * n + j, :, g * HEAD_SIZE : (g + 1) * HEAD_SIZE] = done[g * ROWS : (g + 1) * ROWS]
        for j in range(2):
            remote(
                o.at[2 * n + j], mine, send.at[2 * n + j], recv.at[z], device(xn, 2 * u + j, y, c)
            ).start()

    for d in range(NZ):
        at = lax.rem(z + d, NZ)
        ref = out.at[:, pl.ds(pl.multiple_of(at * WIDTH, WIDTH), WIDTH)]
        remote(ref, ref, send.at[d], recv.at[at], device(xn, z, y, c)).wait_recv()
    for n in range(NZ):
        remote(o.at[n], mine, send.at[n], recv.at[z], device(xn, z, y, c)).wait_send()
    mark.wait()


def per_device(hidden, queries, key_value_weight, doc_ids, scored):
    first_row = lax.axis_index("ctx") * ROWS
    positions = first_row + jnp.arange(ROWS, dtype=jnp.int32)
    half = HEAD_SIZE // 2
    frequency = ROPE_BASE ** (-jnp.arange(half, dtype=jnp.float32) * 2.0 / HEAD_SIZE)
    angles = positions.astype(jnp.float32)[:, None] * frequency[None, :]
    dma = pltpu.SemaphoreType.DMA
    steps = MODEL_WIDTH // DEPTH_STEP
    kv, q8 = pl.pallas_call(
        gather,
        in_specs=[ANY, ANY, ANY, VMEM, VMEM],
        out_specs=[ANY] * 2,
        out_shape=[
            jax.ShapeDtypeStruct((NC, NY, NZ, 2, ROWS, HEAD_SIZE), jnp.bfloat16),
            jax.ShapeDtypeStruct((NZ, ROWS, WIDTH), jnp.bfloat16),
        ],
        scratch_shapes=[
            pltpu.VMEM((MODEL_WIDTH, 1024), jnp.bfloat16),
            pltpu.VMEM((ROWS, MODEL_WIDTH), jnp.bfloat16),
            pltpu.VMEM((KEY_VALUE_HEADS, 2, ROWS, HEAD_SIZE), jnp.bfloat16),
            pltpu.VMEM((ROWS, 1024), jnp.float32),
            pltpu.VMEM((ROWS, WIDTH), jnp.bfloat16),
            dma((steps,)), dma((4,)),
            dma((NZ,)), dma((NZ,)), dma((NZ,)), dma((NZ,)),
            dma((2, NZ)), dma((2, NZ)), dma((2, NZ)), dma((2, NZ)), dma((NY, NZ)), dma((NY, NZ)),
        ],
        compiler_params=pltpu.CompilerParams(
            collective_id=0, has_side_effects=True, vmem_limit_bytes=40 << 20
        ),
        name="gather",
    )(hidden, key_value_weight, queries, jnp.cos(angles), jnp.sin(angles))

    back, marks = pl.pallas_call(
        attend,
        in_specs=[ANY, VMEM, VMEM, ANY],
        out_specs=[ANY] * 2,
        out_shape=[
            jax.ShapeDtypeStruct((ROWS, NZ * WIDTH), jnp.bfloat16),
            jax.ShapeDtypeStruct(scored.shape, jnp.int32),
        ],
        scratch_shapes=[
            pltpu.VMEM((NZ, UNIT, 2 * HEAD_SIZE), jnp.bfloat16),
            pltpu.VMEM((NZ, 2 * HEAD_SIZE, CHUNK), jnp.bfloat16),
            pltpu.VMEM((NZ, CHUNK, 2 * HEAD_SIZE), jnp.bfloat16),
            pltpu.VMEM((2, UNIT, 2 * HEAD_SIZE), jnp.float32),
            pltpu.VMEM((2, UNIT, HEAD_SIZE), jnp.float32),
            pltpu.VMEM((NZ, ROWS, WIDTH), jnp.bfloat16),
            dma((2 * NY * NC,)), dma((NZ,)), dma((NZ,)), dma, dma,
        ],
        compiler_params=pltpu.CompilerParams(
            collective_id=1, has_side_effects=True, vmem_limit_bytes=50 << 20
        ),
        name="attend",
    )(kv, q8, doc_ids, scored)
    return (back * marks[0].astype(jnp.bfloat16)[:, None])[None]


def solution(mesh):
    placed = (
        P("phase", "ctx", None),
        P("phase", "ctx", None),
        P("phase", None, None),
        P("phase", None),
        P("phase", "ctx"),
    )
    return jax.shard_map(
        per_device, mesh=mesh, in_specs=placed, out_specs=P("phase", "ctx", None), check_vma=False
    )
```

```python
import math

import jax
import jax.numpy as jnp
from jax import lax
from jax.experimental import pallas as pl
from jax.experimental.pallas import tpu as pltpu
from jax.sharding import PartitionSpec as P

KEY_VALUE_HEADS = 4
HEAD_SIZE = 128
ROPE_BASE = 500000.0
PHASES = 4
NZ, NY, NC = 8, 4, 2
ROWS = 128
MODEL_WIDTH = 4096
DEPTH_STEP = 512
MESH = pl.DeviceIdType.MESH
FAR = -float(2.0**100)
SCALE = math.log2(math.e) / math.sqrt(HEAD_SIZE)
ORDER = (0, 1, 7, 2, 6, 3, 5, 4)
WIDTH = 2 * HEAD_SIZE
CHUNK = NC * NY * ROWS
ANY = pl.BlockSpec(memory_space=pl.ANY)
VMEM = pl.BlockSpec(memory_space=pltpu.VMEM)


def place():
    x = lax.axis_index("phase")
    at = lax.axis_index("ctx")
    z = at // (NY * NC)
    y = lax.rem(at // NC, NY)
    c = lax.rem(at, NC)
    return x, z, y, c


def device(x, z, y, c):
    return (x, (z * NY + y) * NC + c)


def remote(src, dst, send, recv, who):
    return pltpu.make_async_remote_copy(
        src_ref=src, dst_ref=dst, send_sem=send, recv_sem=recv, device_id=who, device_id_type=MESH
    )


def gather(
    hidden, weight, q, cos_ref, sin_ref, kv, q8,
    wbuf, hbuf, kvp, acc, own, w_sem, l_sem,
    a_send, a_recv, q_send, q_recv, up_send, up_recv, dn_send, dn_recv, p_send, p_recv,
):
    x, z, y, c = place()
    yu, yd = lax.rem(y + 1, NY), lax.rem(y + NY - 1, NY)
    fetch = pltpu.make_async_copy(hidden.at[0], hbuf, l_sem.at[3])
    fetch.start()
    loads = []
    for i in range(MODEL_WIDTH // DEPTH_STEP):
        part = pl.ds(i * DEPTH_STEP, DEPTH_STEP)
        load = pltpu.make_async_copy(weight.at[0, part], wbuf.at[part], w_sem.at[i])
        load.start()
        loads.append(load)
    barrier = pltpu.get_barrier_semaphore()
    for d in range(1, NZ):
        pl.semaphore_signal(
            barrier, inc=1, device_id=device(x, lax.rem(z + d, NZ), y, c), device_id_type=MESH
        )
    for who in (device(x, z, yu, c), device(x, z, yd, c), device(x, z, y, 1 - c)):
        pl.semaphore_signal(barrier, inc=1, device_id=who, device_id_type=MESH)
    pl.semaphore_wait(barrier, NZ - 1 + 3)

    started = []

    def go(copy):
        copy.start()
        started.append(copy)

    def columns(at):
        return q.at[0, :, pl.ds(pl.multiple_of(at * WIDTH, WIDTH), WIDTH)]

    def ask(d):
        to = lax.rem(z + d, NZ)
        go(remote(columns(to), q8.at[z], q_send.at[d], q_recv.at[z], device(x, to, y, c)))

    for d in (4, 3, 5):
        ask(d)
    keep = pltpu.make_async_copy(columns(z), own, l_sem.at[0])
    keep.start()

    fetch.wait()
    wide = hbuf[...].astype(jnp.float32)
    scale = lax.rsqrt(jnp.mean(wide * wide, axis=-1, keepdims=True) + 1e-05)
    rows = (wide * scale).astype(jnp.bfloat16)
    for i, load in enumerate(loads):
        load.wait()
        term = jnp.dot(
            rows[:, i * DEPTH_STEP : (i + 1) * DEPTH_STEP],
            wbuf[i * DEPTH_STEP : (i + 1) * DEPTH_STEP, :],
            preferred_element_type=jnp.float32,
        )
        if i == 0:
            acc[...] = term
        else:
            acc[...] += term
    cos, sin = cos_ref[...], sin_ref[...]
    half = HEAD_SIZE // 2
    for h in range(KEY_VALUE_HEADS):
        keys = acc[:, h * HEAD_SIZE : (h + 1) * HEAD_SIZE]
        low, high = keys[:, :half], keys[:, half:]
        turned = jnp.concatenate([low * cos - high * sin, high * cos + low * sin], axis=-1)
        kvp[h, 0] = jnp.transpose(turned).astype(jnp.bfloat16)
        at = (KEY_VALUE_HEADS + h) * HEAD_SIZE
        kvp[h, 1] = acc[:, at : at + HEAD_SIZE].astype(jnp.bfloat16)

    keep.wait()
    put = pltpu.make_async_copy(own, q8.at[z], l_sem.at[1])
    put.start()

    for d in ORDER[1:]:
        to = lax.rem(z + d, NZ)
        go(remote(kvp.at[to // 2], kv.at[c, y, z], a_send.at[d], a_recv.at[z], device(x, to, y, c)))
    for d in (2, 6, 1, 7):
        ask(d)
    mine = kvp.at[z // 2]
    home = pltpu.make_async_copy(mine, kv.at[c, y, z], l_sem.at[2])
    home.start()

    def slot(r, d):
        return kv.at[c, lax.rem(y + r + NY, NY), lax.rem(z + d, NZ)]

    def arrived(ref, sem):
        remote(ref, ref, sem, sem, device(x, z, y, 1 - c)).wait_recv()

    def partner(r, d, ref=None):
        i = (r + NY) % NY
        src = slot(r, d) if ref is None else ref
        go(remote(src, slot(r, d), p_send.at[i, d], p_recv.at[i, d], device(x, z, y, 1 - c)))

    def up(k, d, ref=None):
        dst = slot(1 - k, d)
        src = dst if ref is None else ref
        go(remote(src, dst, up_send.at[k - 1, d], up_recv.at[k - 1, d], device(x, z, yu, c)))

    def down(k, d, ref=None):
        dst = slot(k - 1, d)
        src = dst if ref is None else ref
        go(remote(src, dst, dn_send.at[k - 1, d], dn_recv.at[k - 1, d], device(x, z, yd, c)))

    far_up, far_down = ORDER[0::2], ORDER[1::2]
    for d in ORDER:
        if d == 0:
            up(1, d, mine)
            down(1, d, mine)
            partner(0, d, mine)
        else:
            arrived(slot(0, d), a_recv.at[lax.rem(z + d, NZ)])
            up(1, d)
            down(1, d)
            partner(0, d)
    for d in ORDER:
        arrived(slot(-1, d), up_recv.at[0, d])
        if d in far_up:
            up(2, d)
        partner(-1, d)
        arrived(slot(1, d), dn_recv.at[0, d])
        if d in far_down:
            down(2, d)
        partner(1, d)
    for d in ORDER:
        if d in far_up:
            arrived(slot(2, d), up_recv.at[1, d])
        else:
            arrived(slot(2, d), dn_recv.at[1, d])
        partner(2, d)
    for r in range(NY):
        for d in ORDER:
            arrived(kv.at[1 - c, lax.rem(y + r, NY), lax.rem(z + d, NZ)], p_recv.at[r, d])
    for d in ORDER[1:]:
        at = lax.rem(z + d, NZ)
        arrived(q8.at[at], q_recv.at[at])
    put.wait()
    home.wait()
    for copy in started:
        copy.wait_send()


UNIT = 2 * ROWS


def attend(
    kv, q8, docs, scored, out, marks,
    qaug, kaug, vaug, acc, top, o, l_sem, send, recv, s_send, s_recv,
):
    x, z, y, c = place()
    xn, xp = lax.rem(x + 1, PHASES), lax.rem(x + PHASES - 1, PHASES)
    loads = []
    for p in range(NY):
        for c2 in range(NC):
            b = p * NC + c2
            keys = pl.ds(b * ROWS, ROWS)
            for part, dst in ((0, kaug.at[:, :HEAD_SIZE, keys]), (1, vaug.at[:, keys, :HEAD_SIZE])):
                load = pltpu.make_async_copy(kv.at[c2, p, :, part], dst, l_sem.at[2 * b + part])
                load.start()
                loads.append(load)
    barrier = pltpu.get_barrier_semaphore()
    for d in range(NZ):
        pl.semaphore_signal(
            barrier, inc=1, device_id=device(xp, lax.rem(z + d, NZ), y, c), device_id_type=MESH
        )
    lanes = lax.broadcasted_iota(jnp.int32, (ROWS, ROWS), 1)
    sublanes = lax.broadcasted_iota(jnp.int32, (ROWS, ROWS), 0)
    apart = jnp.where(lanes == sublanes, 0.0, FAR).astype(jnp.bfloat16)
    block = y * NC + c

    @pl.loop(0, NZ)
    def _(i):
        at = pl.multiple_of(i * CHUNK + block * ROWS, ROWS)
        hot = (sublanes == docs[:, pl.ds(at, ROWS)]).astype(jnp.bfloat16)
        away = lax.dot_general(
            hot, apart, (((0,), (0,)), ((), ())), preferred_element_type=jnp.float32
        ).astype(jnp.bfloat16)
        for g in range(2):
            qaug[i, g * ROWS : (g + 1) * ROWS, :HEAD_SIZE] = q8[i, :, g * HEAD_SIZE : (g + 1) * HEAD_SIZE]
            qaug[i, g * ROWS : (g + 1) * ROWS, HEAD_SIZE:] = away
        vaug[i, :, HEAD_SIZE:] = jnp.ones((CHUNK, HEAD_SIZE), jnp.bfloat16)
        for b in range(NY * NC):
            at = pl.multiple_of(i * CHUNK + b * ROWS, ROWS)
            kaug[i, HEAD_SIZE:, b * ROWS : (b + 1) * ROWS] = (
                sublanes == docs[:, pl.ds(at, ROWS)]
            ).astype(jnp.bfloat16)

    for load in loads:
        load.wait()
    pl.semaphore_wait(barrier, NZ)
    mark = remote(scored, marks, s_send, s_recv, device(xn, z, y, c))
    mark.start()

    def scores(i, k):
        return jnp.dot(qaug[i], kaug[k], preferred_element_type=jnp.float32)

    def first(i):
        s = scores(i, i)
        key = lax.broadcasted_iota(jnp.int32, (1, CHUNK), 1)
        row = lax.broadcasted_iota(jnp.int32, (UNIT, 1), 0)
        s = jnp.where(key <= block * ROWS + lax.rem(row, ROWS), s, -1e30)
        m = jnp.max(s, axis=-1, keepdims=True)
        w = jnp.exp2((s - m) * SCALE).astype(jnp.bfloat16)
        return m, jnp.dot(w, vaug[i], preferred_element_type=jnp.float32)

    def later(i, k, before):
        s = scores(i, k)
        m = jnp.maximum(before, jnp.max(s, axis=-1, keepdims=True))
        w = jnp.exp2((s - m) * SCALE).astype(jnp.bfloat16)
        return m, jnp.exp2((before - m) * SCALE), jnp.dot(w, vaug[k], preferred_element_type=jnp.float32)

    def keep(j, m, total):
        acc[j] = total
        top[j] = jnp.broadcast_to(m, (UNIT, HEAD_SIZE))

    mine = out.at[:, pl.ds(pl.multiple_of(z * WIDTH, WIDTH), WIDTH)]

    @pl.loop(0, NZ // 2)
    def _(n):
        u = lax.rem(z // 2 + n, NZ // 2)
        even, odd = 2 * u, 2 * u + 1
        m0, t0 = first(even)
        m1, t1 = first(odd)
        m1, fade, more = later(odd, even, m1)
        keep(0, m0, t0)
        keep(1, m1, t1 * fade + more)

        @pl.loop(0, even)
        def _(k):
            m0, f0, t0 = later(even, k, top[0][:, :1])
            m1, f1, t1 = later(odd, k, top[1][:, :1])
            keep(0, m0, acc[0] * f0 + t0)
            keep(1, m1, acc[1] * f1 + t1)

        for j in range(2):
            done = (acc[j][:, :HEAD_SIZE] / acc[j][:, HEAD_SIZE:]).astype(jnp.bfloat16)
            for g in range(2):
                o[2 * n + j, :, g * HEAD_SIZE : (g + 1) * HEAD_SIZE] = done[g * ROWS : (g + 1) * ROWS]
        for j in range(2):
            remote(
                o.at[2 * n + j], mine, send.at[2 * n + j], recv.at[z], device(xn, 2 * u + j, y, c)
            ).start()

    for d in range(NZ):
        at = lax.rem(z + d, NZ)
        ref = out.at[:, pl.ds(pl.multiple_of(at * WIDTH, WIDTH), WIDTH)]
        remote(ref, ref, send.at[d], recv.at[at], device(xn, z, y, c)).wait_recv()
    for n in range(NZ):
        remote(o.at[n], mine, send.at[n], recv.at[z], device(xn, z, y, c)).wait_send()
    mark.wait()


def per_device(hidden, queries, key_value_weight, doc_ids, scored):
    first_row = lax.axis_index("ctx") * ROWS
    positions = first_row + jnp.arange(ROWS, dtype=jnp.int32)
    half = HEAD_SIZE // 2
    frequency = ROPE_BASE ** (-jnp.arange(half, dtype=jnp.float32) * 2.0 / HEAD_SIZE)
    angles = positions.astype(jnp.float32)[:, None] * frequency[None, :]
    dma = pltpu.SemaphoreType.DMA
    steps = MODEL_WIDTH // DEPTH_STEP
    kv, q8 = pl.pallas_call(
        gather,
        in_specs=[ANY, ANY, ANY, VMEM, VMEM],
        out_specs=[ANY] * 2,
        out_shape=[
            jax.ShapeDtypeStruct((NC, NY, NZ, 2, ROWS, HEAD_SIZE), jnp.bfloat16),
            jax.ShapeDtypeStruct((NZ, ROWS, WIDTH), jnp.bfloat16),
        ],
        scratch_shapes=[
            pltpu.VMEM((MODEL_WIDTH, 1024), jnp.bfloat16),
            pltpu.VMEM((ROWS, MODEL_WIDTH), jnp.bfloat16),
            pltpu.VMEM((KEY_VALUE_HEADS, 2, ROWS, HEAD_SIZE), jnp.bfloat16),
            pltpu.VMEM((ROWS, 1024), jnp.float32),
            pltpu.VMEM((ROWS, WIDTH), jnp.bfloat16),
            dma((steps,)), dma((4,)),
            dma((NZ,)), dma((NZ,)), dma((NZ,)), dma((NZ,)),
            dma((2, NZ)), dma((2, NZ)), dma((2, NZ)), dma((2, NZ)), dma((NY, NZ)), dma((NY, NZ)),
        ],
        compiler_params=pltpu.CompilerParams(
            collective_id=0, has_side_effects=True, vmem_limit_bytes=66781184
        ),
        name="gather",
    )(hidden, key_value_weight, queries, jnp.cos(angles), jnp.sin(angles))

    back, marks = pl.pallas_call(
        attend,
        in_specs=[ANY, VMEM, VMEM, ANY],
        out_specs=[ANY] * 2,
        out_shape=[
            jax.ShapeDtypeStruct((ROWS, NZ * WIDTH), jnp.bfloat16),
            jax.ShapeDtypeStruct(scored.shape, jnp.int32),
        ],
        scratch_shapes=[
            pltpu.VMEM((NZ, UNIT, 2 * HEAD_SIZE), jnp.bfloat16),
            pltpu.VMEM((NZ, 2 * HEAD_SIZE, CHUNK), jnp.bfloat16),
            pltpu.VMEM((NZ, CHUNK, 2 * HEAD_SIZE), jnp.bfloat16),
            pltpu.VMEM((2, UNIT, 2 * HEAD_SIZE), jnp.float32),
            pltpu.VMEM((2, UNIT, HEAD_SIZE), jnp.float32),
            pltpu.VMEM((NZ, ROWS, WIDTH), jnp.bfloat16),
            dma((2 * NY * NC,)), dma((NZ,)), dma((NZ,)), dma, dma,
        ],
        compiler_params=pltpu.CompilerParams(
            collective_id=1, has_side_effects=True, vmem_limit_bytes=66781184
        ),
        name="attend",
    )(kv, q8, doc_ids, scored)
    return (back * marks[0].astype(jnp.bfloat16)[:, None])[None]


def solution(mesh):
    placed = (
        P("phase", "ctx", None),
        P("phase", "ctx", None),
        P("phase", None, None),
        P("phase", None),
        P("phase", "ctx"),
    )
    return jax.shard_map(
        per_device, mesh=mesh, in_specs=placed, out_specs=P("phase", "ctx", None), check_vma=False
    )
```

```python
import math

import jax
import jax.numpy as jnp
from jax import lax
from jax.experimental import pallas as pl
from jax.experimental.pallas import tpu as pltpu
from jax.sharding import PartitionSpec as P

KEY_VALUE_HEADS = 4
HEAD_SIZE = 128
ROPE_BASE = 500000.0
PHASES = 4
NZ, NY, NC = 8, 4, 2
ROWS = 128
MODEL_WIDTH = 4096
DEPTH_STEP = 512
MESH = pl.DeviceIdType.MESH
FAR = -float(2.0**100)
SCALE = math.log2(math.e) / math.sqrt(HEAD_SIZE)
ORDER = (0, 1, 7, 2, 6, 3, 5, 4)
WIDTH = 2 * HEAD_SIZE
CHUNK = NC * NY * ROWS
ANY = pl.BlockSpec(memory_space=pl.ANY)
VMEM = pl.BlockSpec(memory_space=pltpu.VMEM)


def place():
    x = lax.axis_index("phase")
    at = lax.axis_index("ctx")
    z = at // (NY * NC)
    y = lax.rem(at // NC, NY)
    c = lax.rem(at, NC)
    return x, z, y, c


def device(x, z, y, c):
    return (x, (z * NY + y) * NC + c)


def remote(src, dst, send, recv, who):
    return pltpu.make_async_remote_copy(
        src_ref=src, dst_ref=dst, send_sem=send, recv_sem=recv, device_id=who, device_id_type=MESH
    )


def gather(
    hidden, weight, q, cos_ref, sin_ref, kv, q8,
    wbuf, hbuf, kvp, acc, own, w_sem, l_sem,
    a_send, a_recv, q_send, q_recv, up_send, up_recv, dn_send, dn_recv, p_send, p_recv,
):
    x, z, y, c = place()
    yu, yd = lax.rem(y + 1, NY), lax.rem(y + NY - 1, NY)
    fetch = pltpu.make_async_copy(hidden.at[0], hbuf, l_sem.at[3])
    fetch.start()
    loads = []
    for i in range(MODEL_WIDTH // DEPTH_STEP):
        part = pl.ds(i * DEPTH_STEP, DEPTH_STEP)
        load = pltpu.make_async_copy(weight.at[0, part], wbuf.at[part], w_sem.at[i])
        load.start()
        loads.append(load)
    barrier = pltpu.get_barrier_semaphore()
    for d in range(1, NZ):
        pl.semaphore_signal(
            barrier, inc=1, device_id=device(x, lax.rem(z + d, NZ), y, c), device_id_type=MESH
        )
    for who in (device(x, z, yu, c), device(x, z, yd, c), device(x, z, y, 1 - c)):
        pl.semaphore_signal(barrier, inc=1, device_id=who, device_id_type=MESH)
    pl.semaphore_wait(barrier, NZ - 1 + 3)

    started = []

    def go(copy):
        copy.start()
        started.append(copy)

    def columns(at):
        return q.at[0, :, pl.ds(pl.multiple_of(at * WIDTH, WIDTH), WIDTH)]

    def ask(d):
        to = lax.rem(z + d, NZ)
        go(remote(columns(to), q8.at[z], q_send.at[d], q_recv.at[z], device(x, to, y, c)))

    for d in (4, 3, 5):
        ask(d)
    keep = pltpu.make_async_copy(columns(z), own, l_sem.at[0])
    keep.start()

    fetch.wait()
    wide = hbuf[...].astype(jnp.float32)
    scale = lax.rsqrt(jnp.mean(wide * wide, axis=-1, keepdims=True) + 1e-05)
    rows = (wide * scale).astype(jnp.bfloat16)
    for i, load in enumerate(loads):
        load.wait()
        term = jnp.dot(
            rows[:, i * DEPTH_STEP : (i + 1) * DEPTH_STEP],
            wbuf[i * DEPTH_STEP : (i + 1) * DEPTH_STEP, :],
            preferred_element_type=jnp.float32,
        )
        if i == 0:
            acc[...] = term
        else:
            acc[...] += term
    cos, sin = cos_ref[...], sin_ref[...]
    half = HEAD_SIZE // 2
    for h in range(KEY_VALUE_HEADS):
        keys = acc[:, h * HEAD_SIZE : (h + 1) * HEAD_SIZE]
        low, high = keys[:, :half], keys[:, half:]
        turned = jnp.concatenate([low * cos - high * sin, high * cos + low * sin], axis=-1)
        kvp[h, 0] = jnp.transpose(turned).astype(jnp.bfloat16)
        at = (KEY_VALUE_HEADS + h) * HEAD_SIZE
        kvp[h, 1] = acc[:, at : at + HEAD_SIZE].astype(jnp.bfloat16)

    keep.wait()
    put = pltpu.make_async_copy(own, q8.at[z], l_sem.at[1])
    put.start()

    for d in ORDER[1:]:
        to = lax.rem(z + d, NZ)
        go(remote(kvp.at[to // 2], kv.at[c, y, z], a_send.at[d], a_recv.at[z], device(x, to, y, c)))
    for d in (2, 6, 1, 7):
        ask(d)
    mine = kvp.at[z // 2]
    home = pltpu.make_async_copy(mine, kv.at[c, y, z], l_sem.at[2])
    home.start()

    def slot(r, d):
        return kv.at[c, lax.rem(y + r + NY, NY), lax.rem(z + d, NZ)]

    def arrived(ref, sem):
        remote(ref, ref, sem, sem, device(x, z, y, 1 - c)).wait_recv()

    def partner(r, d, ref=None):
        i = (r + NY) % NY
        src = slot(r, d) if ref is None else ref
        go(remote(src, slot(r, d), p_send.at[i, d], p_recv.at[i, d], device(x, z, y, 1 - c)))

    def up(k, d, ref=None):
        dst = slot(1 - k, d)
        src = dst if ref is None else ref
        go(remote(src, dst, up_send.at[k - 1, d], up_recv.at[k - 1, d], device(x, z, yu, c)))

    def down(k, d, ref=None):
        dst = slot(k - 1, d)
        src = dst if ref is None else ref
        go(remote(src, dst, dn_send.at[k - 1, d], dn_recv.at[k - 1, d], device(x, z, yd, c)))

    far_up, far_down = ORDER[0::2], ORDER[1::2]
    for d in ORDER:
        if d == 0:
            up(1, d, mine)
            down(1, d, mine)
            partner(0, d, mine)
        else:
            arrived(slot(0, d), a_recv.at[lax.rem(z + d, NZ)])
            up(1, d)
            down(1, d)
            partner(0, d)
    for d in ORDER:
        arrived(slot(-1, d), up_recv.at[0, d])
        if d in far_up:
            up(2, d)
        partner(-1, d)
        arrived(slot(1, d), dn_recv.at[0, d])
        if d in far_down:
            down(2, d)
        partner(1, d)
    for d in ORDER:
        if d in far_up:
            arrived(slot(2, d), up_recv.at[1, d])
        else:
            arrived(slot(2, d), dn_recv.at[1, d])
        partner(2, d)
    for r in range(NY):
        for d in ORDER:
            arrived(kv.at[1 - c, lax.rem(y + r, NY), lax.rem(z + d, NZ)], p_recv.at[r, d])
    for d in ORDER[1:]:
        at = lax.rem(z + d, NZ)
        arrived(q8.at[at], q_recv.at[at])
    put.wait()
    home.wait()
    for copy in started:
        copy.wait_send()


UNIT = 2 * ROWS


def attend(
    kv, q8, docs, scored, out, marks,
    qaug, kaug, vaug, acc, top, o, l_sem, send, recv, s_send, s_recv,
):
    x, z, y, c = place()
    xn, xp = lax.rem(x + 1, PHASES), lax.rem(x + PHASES - 1, PHASES)
    loads = []
    for p in range(NY):
        for c2 in range(NC):
            b = p * NC + c2
            keys = pl.ds(b * ROWS, ROWS)
            for part, dst in ((0, kaug.at[:, :HEAD_SIZE, keys]), (1, vaug.at[:, keys, :HEAD_SIZE])):
                load = pltpu.make_async_copy(kv.at[c2, p, :, part], dst, l_sem.at[2 * b + part])
                load.start()
                loads.append(load)
    barrier = pltpu.get_barrier_semaphore()
    for d in range(NZ):
        pl.semaphore_signal(
            barrier, inc=1, device_id=device(xp, lax.rem(z + d, NZ), y, c), device_id_type=MESH
        )
    lanes = lax.broadcasted_iota(jnp.int32, (ROWS, ROWS), 1)
    sublanes = lax.broadcasted_iota(jnp.int32, (ROWS, ROWS), 0)
    apart = jnp.where(lanes == sublanes, 0.0, FAR).astype(jnp.bfloat16)
    block = y * NC + c

    @pl.loop(0, NZ)
    def _(i):
        at = pl.multiple_of(i * CHUNK + block * ROWS, ROWS)
        hot = (sublanes == docs[:, pl.ds(at, ROWS)]).astype(jnp.bfloat16)
        away = lax.dot_general(
            hot, apart, (((0,), (0,)), ((), ())), preferred_element_type=jnp.float32
        ).astype(jnp.bfloat16)
        for g in range(2):
            qaug[i, g * ROWS : (g + 1) * ROWS, :HEAD_SIZE] = q8[i, :, g * HEAD_SIZE : (g + 1) * HEAD_SIZE]
            qaug[i, g * ROWS : (g + 1) * ROWS, HEAD_SIZE:] = away
        vaug[i, :, HEAD_SIZE:] = jnp.ones((CHUNK, HEAD_SIZE), jnp.bfloat16)
        for b in range(NY * NC):
            at = pl.multiple_of(i * CHUNK + b * ROWS, ROWS)
            kaug[i, HEAD_SIZE:, b * ROWS : (b + 1) * ROWS] = (
                sublanes == docs[:, pl.ds(at, ROWS)]
            ).astype(jnp.bfloat16)

    for load in loads:
        load.wait()
    pl.semaphore_wait(barrier, NZ)
    mark = remote(scored, marks, s_send, s_recv, device(xn, z, y, c))
    mark.start()

    def scores(i, k):
        return jnp.dot(qaug[i], kaug[k], preferred_element_type=jnp.float32)

    def first(i):
        s = scores(i, i)
        key = lax.broadcasted_iota(jnp.int32, (1, CHUNK), 1)
        row = lax.broadcasted_iota(jnp.int32, (UNIT, 1), 0)
        s = jnp.where(key <= block * ROWS + lax.rem(row, ROWS), s, -1e30)
        m = jnp.max(s, axis=-1, keepdims=True)
        w = jnp.exp2((s - m) * SCALE).astype(jnp.bfloat16)
        return m, jnp.dot(w, vaug[i], preferred_element_type=jnp.float32)

    def later(i, k, before):
        s = scores(i, k)
        m = jnp.maximum(before, jnp.max(s, axis=-1, keepdims=True))
        w = jnp.exp2((s - m) * SCALE).astype(jnp.bfloat16)
        return m, jnp.exp2((before - m) * SCALE), jnp.dot(w, vaug[k], preferred_element_type=jnp.float32)

    def keep(j, m, total):
        acc[j] = total
        top[j] = jnp.broadcast_to(m, (UNIT, HEAD_SIZE))

    mine = out.at[:, pl.ds(pl.multiple_of(z * WIDTH, WIDTH), WIDTH)]

    @pl.loop(0, NZ // 2)
    def _(n):
        u = lax.rem(z // 2 + n, NZ // 2)
        even, odd = 2 * u, 2 * u + 1
        m0, t0 = first(even)
        m1, t1 = first(odd)
        m1, fade, more = later(odd, even, m1)
        keep(0, m0, t0)
        keep(1, m1, t1 * fade + more)

        @pl.loop(0, even)
        def _(k):
            m0, f0, t0 = later(even, k, top[0][:, :1])
            m1, f1, t1 = later(odd, k, top[1][:, :1])
            keep(0, m0, acc[0] * f0 + t0)
            keep(1, m1, acc[1] * f1 + t1)

        for j in range(2):
            done = (acc[j][:, :HEAD_SIZE] / acc[j][:, HEAD_SIZE:]).astype(jnp.bfloat16)
            for g in range(2):
                o[2 * n + j, :, g * HEAD_SIZE : (g + 1) * HEAD_SIZE] = done[g * ROWS : (g + 1) * ROWS]
        for j in range(2):
            remote(
                o.at[2 * n + j], mine, send.at[2 * n + j], recv.at[z], device(xn, 2 * u + j, y, c)
            ).start()

    for d in range(NZ):
        at = lax.rem(z + d, NZ)
        ref = out.at[:, pl.ds(pl.multiple_of(at * WIDTH, WIDTH), WIDTH)]
        remote(ref, ref, send.at[d], recv.at[at], device(xn, z, y, c)).wait_recv()
    for n in range(NZ):
        remote(o.at[n], mine, send.at[n], recv.at[z], device(xn, z, y, c)).wait_send()
    mark.wait()


def per_device(hidden, queries, key_value_weight, doc_ids, scored):
    first_row = lax.axis_index("ctx") * ROWS
    positions = first_row + jnp.arange(ROWS, dtype=jnp.int32)
    half = HEAD_SIZE // 2
    frequency = ROPE_BASE ** (-jnp.arange(half, dtype=jnp.float32) * 2.0 / HEAD_SIZE)
    angles = positions.astype(jnp.float32)[:, None] * frequency[None, :]
    dma = pltpu.SemaphoreType.DMA
    steps = MODEL_WIDTH // DEPTH_STEP
    kv, q8 = pl.pallas_call(
        gather,
        in_specs=[ANY, ANY, ANY, VMEM, VMEM],
        out_specs=[ANY] * 2,
        out_shape=[
            jax.ShapeDtypeStruct((NC, NY, NZ, 2, ROWS, HEAD_SIZE), jnp.bfloat16),
            jax.ShapeDtypeStruct((NZ, ROWS, WIDTH), jnp.bfloat16),
        ],
        scratch_shapes=[
            pltpu.VMEM((MODEL_WIDTH, 1024), jnp.bfloat16),
            pltpu.VMEM((ROWS, MODEL_WIDTH), jnp.bfloat16),
            pltpu.VMEM((KEY_VALUE_HEADS, 2, ROWS, HEAD_SIZE), jnp.bfloat16),
            pltpu.VMEM((ROWS, 1024), jnp.float32),
            pltpu.VMEM((ROWS, WIDTH), jnp.bfloat16),
            dma((steps,)), dma((4,)),
            dma((NZ,)), dma((NZ,)), dma((NZ,)), dma((NZ,)),
            dma((2, NZ)), dma((2, NZ)), dma((2, NZ)), dma((2, NZ)), dma((NY, NZ)), dma((NY, NZ)),
        ],
        compiler_params=pltpu.CompilerParams(
            collective_id=0, has_side_effects=True, vmem_limit_bytes=40 << 20
        ),
        name="gather",
    )(hidden, key_value_weight, queries, jnp.cos(angles), jnp.sin(angles))

    back, marks = pl.pallas_call(
        attend,
        in_specs=[ANY, VMEM, VMEM, ANY],
        out_specs=[ANY] * 2,
        out_shape=[
            jax.ShapeDtypeStruct((ROWS, NZ * WIDTH), jnp.bfloat16),
            jax.ShapeDtypeStruct(scored.shape, jnp.int32),
        ],
        scratch_shapes=[
            pltpu.VMEM((NZ, UNIT, 2 * HEAD_SIZE), jnp.bfloat16),
            pltpu.VMEM((NZ, 2 * HEAD_SIZE, CHUNK), jnp.bfloat16),
            pltpu.VMEM((NZ, CHUNK, 2 * HEAD_SIZE), jnp.bfloat16),
            pltpu.VMEM((2, UNIT, 2 * HEAD_SIZE), jnp.float32),
            pltpu.VMEM((2, UNIT, HEAD_SIZE), jnp.float32),
            pltpu.VMEM((NZ, ROWS, WIDTH), jnp.bfloat16),
            dma((2 * NY * NC,)), dma((NZ,)), dma((NZ,)), dma, dma,
        ],
        compiler_params=pltpu.CompilerParams(
            collective_id=1, has_side_effects=True, vmem_limit_bytes=32 << 20
        ),
        name="attend",
    )(kv, q8, doc_ids, scored)
    return (back * marks[0].astype(jnp.bfloat16)[:, None])[None]


def solution(mesh):
    placed = (
        P("phase", "ctx", None),
        P("phase", "ctx", None),
        P("phase", None, None),
        P("phase", None),
        P("phase", "ctx"),
    )
    return jax.shard_map(
        per_device, mesh=mesh, in_specs=placed, out_specs=P("phase", "ctx", None), check_vma=False
    )
```
